32 devices in a mesh: sweep: 2 (over y), tm: 4 (over z), height: 2 (over x), width: 2 (over core).
Axes of the slice: x: 2, y: 2, z: 4, core: 2. Of those that a mesh axis runs over, the one named last changes fastest.
Arguments:
- queries: bfloat16 [8, 2, 4, 64, 2560], P(('sweep', 'tm'), 'height', 'width'), parts along dimension 0, may hold values from -8 to 8
- keys: bfloat16 [8, 2, 4, 64, 2560], P(('sweep', 'tm'), 'height', 'width'), parts along dimension 0, may hold values from -8 to 8
- values: bfloat16 [8, 2, 4, 64, 2560], P(('sweep', 'tm'), 'height', 'width'), parts along dimension 0, may hold values from -6 to 6
- windows: int32 [20, 3], replicated, may hold values from 0 to 1, as said below
- tile_mask: int32 [4, 2, 4, 27], P('tm', 'height', 'width'), may hold values 0 or 1
- coefficient: float32 [2], P('sweep'), parts along dimension 0, may hold values from 0.5 to 1.5
- layer: int32 [2], P('sweep'), parts along dimension 0, may hold values from 0 to 39
- steering: bfloat16 [40, 2560], replicated, may hold values from -4 to 4
Outputs:
- attended: bfloat16 [8, 2, 4, 64, 2560], P(('sweep', 'tm'), 'height', 'width'), parts along dimension 0
The draws below stay inside these ranges and needn't reach their ends.
There are 2 independent parts, one for each index of `sweep`. The reference program is written for one: setup_inputs(seed, part) draws one part's arguments, and reference() takes and returns one part's arrays. A program takes and returns all parts, laid end to end along the dimension named above; an argument that names none is the same for every part. Nothing has to cross between parts.
Inputs may be any that keep to these rules, and one draw needn't show every extreme that they name: `windows`: some head reaches one tile along all three dimensions.
All inputs are finite; a program needn't handle non-finite values. No bound on the sum of `tile_mask` on one device may be relied on, other than what follows from the above.
Results may differ from the reference program's by a relative error of at most 0.0045.
Values may be sent and summed in bfloat16 or wider, within the bound.
A program may use at most 192 MiB of HBM per device.

```python
import math
import jax
import jax.numpy as jnp
from jax import lax

H = 20
DH = 128
HD = 2560
TILE_TOK = 64
LAYERS = 40
NT_F = 4
NT_R = 2
NT_C = 4


def drawn_pair(key):
    shape = (NT_F, NT_R, NT_C, TILE_TOK, H, DH)
    query_base = jnp.clip(1.5 * jax.random.normal(jax.random.fold_in(key, 21), shape, jnp.float32), -8.0, 8.0)
    key_base = jnp.clip(1.5 * jax.random.normal(jax.random.fold_in(key, 22), shape, jnp.float32), -8.0, 8.0)
    flat = (NT_F, NT_R, NT_C, TILE_TOK, H * DH)
    return (query_base.reshape(flat), key_base.reshape(flat))


def draw_queries(key, part):
    return drawn_pair(key)[0].astype(jnp.bfloat16)


def draw_keys(key, part):
    return drawn_pair(key)[1].astype(jnp.bfloat16)


def draw_windows(key, part):
    reach = jax.random.randint(jax.random.fold_in(key, 11), (H, 3), 0, 2).astype(jnp.int32)
    chosen = jax.random.randint(jax.random.fold_in(key, 12), (), 0, H).astype(jnp.int32)
    full = (jnp.arange(H, dtype=jnp.int32) == chosen)[:, None]
    return jnp.where(full, 1, reach).astype(jnp.int32)


def set_ends(entries, key, least, largest):
    spot = [jax.random.randint(jax.random.fold_in(key, axis), (), 0, length) for axis, length in enumerate(entries.shape)]
    widest = entries.shape.index(max(entries.shape))
    beside = spot[:widest] + [(spot[widest] + 1) % entries.shape[widest]] + spot[widest + 1:]
    return entries.at[tuple(spot)].set(least).at[tuple(beside)].set(largest)


def levels(own_key, dims, cuts, least, high):
    def one(dim, shards_of):
        draws = jax.random.uniform(jax.random.fold_in(jax.random.fold_in(own_key, 6), dim), (shards_of,), jnp.float32, least / len(cuts), high / len(cuts))
        return jnp.repeat(jnp.exp(draws), dims[dim] // shards_of).reshape((-1,) + (1,) * (len(dims) - dim - 1))

    factor_of = one(*cuts[0])
    for cut in cuts[1:]:
        factor_of = factor_of * one(*cut)
    return factor_of


def gaussian(rng, extent, width, limit, shards=(), kind=jnp.bfloat16):
    values = jax.random.normal(rng, extent, jnp.float32) * width
    if len(shards) > 0:
        values = levels(rng, extent, shards, -0.22, 0.18) * values
    return jnp.clip(values, min=-limit, max=limit).astype(kind)


def setup_inputs(seed: int = 0, part: int = 0) -> dict:
    arg_keys = jax.random.split(jax.random.key(seed), 9)
    part_keys = jax.random.split(jax.random.fold_in(arg_keys[8], part), 9)
    queries = draw_queries(jax.random.fold_in(jax.random.fold_in(arg_keys[8], part), 71), part)
    keys = draw_keys(jax.random.fold_in(jax.random.fold_in(arg_keys[8], part), 71), part)
    values = gaussian(part_keys[2], (NT_F, NT_R, NT_C, TILE_TOK, HD), 1.0, 6.0, ((0, 4), (1, 2), (2, 2)))
    windows = draw_windows(jax.random.fold_in(arg_keys[8], 71), part)
    tile_mask = set_ends((jax.random.randint(arg_keys[4], (NT_F, NT_R, NT_C, 27), 0, 4) < 3).astype(jnp.int32), jax.random.fold_in(arg_keys[4], 1), 0, 1)
    coefficient = jnp.clip(jax.random.uniform(part_keys[5], (1,), jnp.float32, 0.5, 1.5), 0.5, 1.5)
    layer = jax.random.randint(part_keys[6], (1,), 0, LAYERS).astype(jnp.int32)
    steering = gaussian(arg_keys[7], (LAYERS, HD), 0.3, 4.0)
    return dict(queries=queries, keys=keys, values=values, windows=windows, tile_mask=tile_mask, coefficient=coefficient, layer=layer, steering=steering)


NEG = -1e+30

def allowed_offsets(tile_mask, windows, starts, totals):
    frames, rows, cols = (tile_mask.shape[0], tile_mask.shape[1], tile_mask.shape[2])
    frame_pos = starts[0] + jnp.arange(frames, dtype=jnp.int32)[:, None, None]
    row_pos = starts[1] + jnp.arange(rows, dtype=jnp.int32)[None, :, None]
    col_pos = starts[2] + jnp.arange(cols, dtype=jnp.int32)[None, None, :]
    stacked = []
    for offset in range(27):
        shift_f = offset // 9 - 1
        shift_r = offset // 3 % 3 - 1
        shift_c = offset % 3 - 1
        inside = (frame_pos + shift_f >= 0) & (frame_pos + shift_f < totals[0])
        inside = inside & (row_pos + shift_r >= 0) & (row_pos + shift_r < totals[1])
        inside = inside & (col_pos + shift_c >= 0) & (col_pos + shift_c < totals[2])
        chosen = jnp.logical_or(tile_mask[..., offset] == 1, offset == 13)
        reach = (windows[:, 0] >= abs(shift_f)) & (windows[:, 1] >= abs(shift_r)) & (windows[:, 2] >= abs(shift_c))
        stacked.append(jnp.logical_and((inside & chosen)[..., None], reach))
    return jnp.stack(stacked)

def reference(queries, keys, values, windows, tile_mask, coefficient, layer, steering):
    scale = 1.0 / math.sqrt(DH)
    allowed = allowed_offsets(tile_mask, windows, (0, 0, 0), (NT_F, NT_R, NT_C))
    padding = ((1, 1), (1, 1), (1, 1), (0, 0), (0, 0))

    def one_head(head):
        start = (head * DH).astype(jnp.int32)
        query_head = lax.dynamic_slice_in_dim(queries, start, DH, 4).astype(jnp.float32)
        key_head = jnp.pad(lax.dynamic_slice_in_dim(keys, start, DH, 4).astype(jnp.float32), padding)
        value_head = jnp.pad(lax.dynamic_slice_in_dim(values, start, DH, 4).astype(jnp.float32), padding)
        usable = lax.dynamic_index_in_dim(allowed, head, 4, keepdims=False)[..., None, None]
        scores = []
        for offset in range(27):
            step_f, step_r, step_c = (offset // 9, offset // 3 % 3, offset % 3)
            key_here = key_head[step_f:step_f + NT_F, step_r:step_r + NT_R, step_c:step_c + NT_C]
            scores.append(jnp.einsum('frcid,frcjd->frcij', query_head, key_here))
        scores = jnp.stack(scores) * scale
        masked = jnp.where(usable, scores, NEG)
        top = lax.optimization_barrier(jnp.max(masked, axis=(0, 5), keepdims=True))
        expos = jnp.where(usable, jnp.exp(masked - top), 0.0)
        total = lax.optimization_barrier(jnp.sum(expos, axis=(0, 5), keepdims=True))
        weights = lax.optimization_barrier((expos / total).astype(jnp.bfloat16)).astype(jnp.float32)
        mixture = jnp.zeros(query_head.shape, jnp.float32)
        for offset in range(27):
            step_f, step_r, step_c = (offset // 9, offset // 3 % 3, offset % 3)
            value_here = value_head[step_f:step_f + NT_F, step_r:step_r + NT_R, step_c:step_c + NT_C]
            mixture = mixture + jnp.einsum('frcij,frcjd->frcid', weights[offset], value_here)
        return mixture
    heads_out = lax.map(one_head, jnp.arange(H, dtype=jnp.int32))
    mixture = jnp.transpose(heads_out, (1, 2, 3, 4, 0, 5)).reshape(NT_F, NT_R, NT_C, TILE_TOK, H * DH)
    vector = lax.dynamic_index_in_dim(steering, layer[0], 0, keepdims=False).astype(jnp.float32)
    return (mixture + coefficient[0] * vector).astype(jnp.bfloat16)
```

```python
import functools
import math

import jax
import jax.numpy as jnp
from jax import lax
from jax.experimental import pallas as pl
from jax.experimental.pallas import tpu as pltpu
from jax.sharding import PartitionSpec as P

DH = 128
NEG = -1e30
MESH = pl.DeviceIdType.MESH
HC = 2


def kernel(
    n_tm, n_height, heads,
    q_ref, k_ref, v_ref, win_ref, mask_ref, coef_ref, layer_ref, steer_ref,
    out_ref,
    kbuf, vbuf, qbuf, mbuf, bias, scores, svec, ostage,
    ssem, rsem, lsem, qsem, msem, osem,
):
    tokens = q_ref.shape[0]
    cols = mask_ref.shape[0]
    tile = tokens // cols
    all_cols = 2 * cols
    half = (heads // 2) * DH
    cw = HC * DH
    chunks = half // cw
    c = lax.axis_index("width")
    z = lax.axis_index("tm")
    x = lax.axis_index("height")
    sib = 1 - c
    if n_height == 1:
        rows = []
    elif n_height == 2:
        rows = [(1 - 2 * x, True, 1)]
    else:
        rows = [(-1, x > 0, 2), (1, x < n_height - 1, 1)]
    nr = 1 + len(rows)
    ns = 3 * nr
    frames = [(-1, z > 0, 2), (1, z < n_tm - 1, 1)]
    bufs = ((k_ref, kbuf), (v_ref, vbuf))

    def guard(cond, body):
        if cond is True:
            body()
        else:
            pl.when(cond)(body)

    barrier = pltpu.get_barrier_semaphore()

    def greet(**where):
        pl.semaphore_signal(barrier, inc=1, device_id=where, device_id_type=MESH)

    greet(width=sib)
    expect = jnp.int32(1)
    for d, ok, _ in rows:
        def body(d=d):
            for t in range(2):
                greet(height=x + d, width=jnp.int32(t))
        guard(ok, body)
        expect = expect + (2 if ok is True else 2 * ok.astype(jnp.int32))
    for d, ok, _ in frames:
        def body(d=d):
            for t in range(2):
                greet(tm=z + d, width=jnp.int32(t))
        guard(ok, body)
        expect = expect + 2 * ok.astype(jnp.int32)
    pl.semaphore_wait(barrier, expect)

    def remote(src, dst, s, r, where):
        return pltpu.make_async_remote_copy(
            src_ref=src, dst_ref=dst, send_sem=s, recv_sem=r, device_id=where, device_id_type=MESH
        )

    def columns(core, g):
        return pl.ds(pl.multiple_of(core * half + g * cw, DH), cw)

    def own(kv, dest, g, core, slot, where):
        src, buf = bufs[kv]
        return remote(
            src.at[:, columns(core, g)], buf.at[slot, g, c],
            ssem.at[kv, dest, g, core], rsem.at[kv, slot, g, c], where,
        )

    def to_sibling(kv, g):
        return own(kv, 0, g, sib, 0, dict(width=sib))

    def to_row(kv, i, g, core):
        d, _, there = rows[i]
        return own(kv, 1 + i, g, jnp.int32(core), there, dict(height=x + d, width=jnp.int32(core)))

    def to_frame(kv, i, g, core):
        d, _, there = frames[i]
        return own(kv, nr + i, g, jnp.int32(core), there * nr, dict(tm=z + d, width=jnp.int32(core)))

    def forward(kv, j, i, g):
        d, _, there = frames[i]
        buf = bufs[kv][1]
        return remote(
            buf.at[1 + j, g], buf.at[there * nr + 1 + j, g],
            ssem.at[kv, nr + 2 + 2 * j + i, g, 0], rsem.at[kv, there * nr + 1 + j, g, 0],
            dict(tm=z + d),
        )

    def arrived(kv, slot, g, core):
        src, buf = bufs[kv]
        return remote(
            src.at[:, columns(core, g)], buf.at[slot, g, core],
            ssem.at[kv, 0, g, core], rsem.at[kv, slot, g, core], dict(width=sib),
        )

    def forwarded(kv, slot, g):
        buf = bufs[kv][1]
        return remote(
            buf.at[slot, g], buf.at[slot, g],
            ssem.at[kv, 0, g, 0], rsem.at[kv, slot, g, 0], dict(width=sib),
        )

    def keep(kv, g):
        src, buf = bufs[kv]
        return pltpu.make_async_copy(src.at[:, columns(c, g)], buf.at[0, g, c], lsem.at[kv, g])

    def keep_q(g):
        return pltpu.make_async_copy(q_ref.at[:, columns(c, g)], qbuf.at[g, c], lsem.at[2, g])

    def send_q(g):
        return remote(
            q_ref.at[:, columns(sib, g)], qbuf.at[g, c], qsem.at[0, g], qsem.at[1, g], dict(width=sib)
        )

    def send_mask():
        return remote(mask_ref, mbuf, msem.at[0], msem.at[1], dict(width=sib))

    def row_ok(i):
        return rows[i][1]

    send_mask().start()

    def start_rows(g, _):
        for i in range(nr - 1):
            def body(i=i):
                for core in range(2):
                    for kv in range(2):
                        to_row(kv, i, g, core).start()
            guard(row_ok(i), body)
        return 0

    def start_frames(g):
        for i in range(2):
            def body(i=i):
                for core in range(2):
                    for kv in range(2):
                        to_frame(kv, i, g, core).start()
            guard(frames[i][1], body)

    def start_local(g, _):
        keep_q(g).start()
        send_q(g).start()
        for kv in range(2):
            keep(kv, g).start()
            to_sibling(kv, g).start()
        return 0

    start_rows(0, 0)
    start_frames(0)
    lax.fori_loop(1, chunks, start_rows, 0)
    lax.fori_loop(0, chunks, start_local, 0)

    for i in range(nr - 1):
        if row_ok(i) is not True:
            @pl.when(jnp.logical_not(row_ok(i)))
            def _(i=i):
                for f in range(3):
                    for _, buf in bufs:
                        buf[f * nr + 1 + i] = jnp.zeros(buf.shape[1:], buf.dtype)
    for i in range(2):
        @pl.when(jnp.logical_not(frames[i][1]))
        def _(i=i):
            for j in range(nr):
                for _, buf in bufs:
                    def zero(g, _, j=j, buf=buf):
                        buf[(1 + i) * nr + j, g] = jnp.zeros(buf.shape[2:], buf.dtype)
                        return 0
                    if j == 0 or row_ok(j - 1) is True:
                        lax.fori_loop(0, chunks, zero, 0)
                    else:
                        @pl.when(row_ok(j - 1))
                        def _(zero=zero):
                            lax.fori_loop(0, chunks, zero, 0)

    pick = lax.broadcasted_iota(jnp.int32, (steer_ref.shape[0], DH), 0) == layer_ref[0]
    for h in range(heads):
        rows_f32 = steer_ref[:, h * DH : (h + 1) * DH].astype(jnp.float32)
        svec[h] = coef_ref[0] * jnp.sum(jnp.where(pick, rows_f32, 0.0), axis=0, keepdims=True)

    def pump(g, _):
        @pl.when(g > 0)
        def _():
            start_frames(g)
        for j in range(nr - 1):
            def body(j=j):
                for core in range(2):
                    for kv in range(2):
                        arrived(kv, 1 + j, g, jnp.int32(core)).wait_recv()
                for i in range(2):
                    def inner(i=i):
                        for kv in range(2):
                            forward(kv, j, i, g).start()
                    guard(frames[i][1], inner)
            guard(row_ok(j), body)
        return 0

    lax.fori_loop(0, chunks, pump, 0)

    send_mask().wait_recv()
    theirs = mbuf[...]
    mine = mask_ref[...]
    first = jnp.where(c == 0, mine, theirs)
    second = jnp.where(c == 0, theirs, mine)
    kept = jnp.concatenate([first, second], axis=0)
    span = all_cols * tile
    lane = lax.broadcasted_iota(jnp.int32, (1, kept.shape[1]), 1)
    block = lax.broadcasted_iota(jnp.int32, (1, span), 1) // tile
    for f in range(3):
        df = (0, -1, 1)[f]
        f_ok = True if f == 0 else frames[f - 1][1]
        for r in range(nr):
            dr = 0 if r == 0 else rows[r - 1][0]
            r_ok = True if r == 0 else row_ok(r - 1)
            base = 9 * (df + 1) + 3 * (dr + 1)
            slot = f * nr + r
            ok = None
            for cond in (f_ok, r_ok):
                if cond is not True:
                    ok = cond if ok is None else jnp.logical_and(ok, cond)
            for qc in range(all_cols):
                line = jnp.full((1, span), NEG, jnp.float32)
                for kc in range(max(qc - 1, 0), min(qc + 2, all_cols)):
                    if slot == 0 and kc == qc:
                        value = jnp.zeros((1, 1), jnp.float32)
                    else:
                        here = jnp.where(lane == base + (kc - qc + 1), kept[qc : qc + 1], 0)
                        hit = jnp.sum(here.astype(jnp.float32), axis=1, keepdims=True)
                        value = jnp.where(hit == 1.0, 0.0, NEG)
                        if ok is not None:
                            value = jnp.where(ok, value, NEG)
                    line = jnp.where(block == kc, value, line)
                alone = jnp.where(block == qc, line, NEG)
                at = pl.ds(qc * tile, tile)
                bias[slot, at, :] = jnp.broadcast_to(alone, (tile, span))
                bias[ns + slot, at, :] = jnp.broadcast_to(line, (tile, span))
    bias[2 * ns] = jnp.full((span, span), NEG, jnp.float32)

    scale = 1.0 / math.sqrt(DH)

    def out_home(g):
        return pltpu.make_async_copy(
            ostage.at[g, c], out_ref.at[:, columns(c, g)], lsem.at[3, g]
        )

    def out_away(g):
        return remote(
            ostage.at[g, sib], out_ref.at[:, columns(c, g)], osem.at[0, g], osem.at[1, g], dict(width=sib)
        )

    def out_arrived(g):
        return remote(
            ostage.at[g, sib], out_ref.at[:, columns(sib, g)], osem.at[0, g], osem.at[1, g], dict(width=sib)
        )

    def attend(g, _):
        keep_q(g).wait()
        send_q(g).wait_recv()
        for kv in range(2):
            keep(kv, g).wait()
            arrived(kv, 0, g, sib).wait_recv()
        for i in range(2):
            def body(i=i):
                for kv in range(2):
                    for core in range(2):
                        arrived(kv, (1 + i) * nr, g, jnp.int32(core)).wait_recv()
                    for j in range(nr - 1):
                        def inner(j=j, kv=kv):
                            forwarded(kv, (1 + i) * nr + 1 + j, g).wait_recv()
                        guard(row_ok(j), inner)
            guard(frames[i][1], body)
        for hh in range(HC):
            h = c * (heads // 2) + g * HC + hh
            lanes = slice(hh * DH, (hh + 1) * DH)
            wf, wr, wc = win_ref[h, 0], win_ref[h, 1], win_ref[h, 2]
            q = qbuf[g][:, :, lanes].reshape(span, DH)
            top = None
            for slot in range(ns):
                index = jnp.where(wc >= 1, ns + slot, slot)
                if slot // nr > 0:
                    index = jnp.where(wf >= 1, index, 2 * ns)
                if slot % nr > 0:
                    index = jnp.where(wr >= 1, index, 2 * ns)
                key = kbuf[slot, g][:, :, lanes].reshape(span, DH)
                s = lax.dot_general(
                    q, key, (((1,), (1,)), ((), ())), preferred_element_type=jnp.float32
                )
                s = s * scale + bias[index]
                scores[slot] = s
                high = jnp.maximum(s[:, :DH], s[:, DH:]) if span == 2 * DH else jnp.max(s, axis=1, keepdims=True)
                top = high if top is None else jnp.maximum(top, high)
            top = jnp.max(top, axis=1, keepdims=True)
            total = None
            mixture = None
            for slot in range(ns):
                e = jnp.exp(scores[slot] - top)
                part = e[:, :DH] + e[:, DH:] if span == 2 * DH else jnp.sum(e, axis=1, keepdims=True)
                total = part if total is None else total + part
                value = vbuf[slot, g][:, :, lanes].reshape(span, DH)
                term = jnp.dot(e.astype(jnp.bfloat16), value, preferred_element_type=jnp.float32)
                mixture = term if mixture is None else mixture + term
            total = jnp.sum(total, axis=1, keepdims=True)
            attended = mixture * (1.0 / total) + svec[h]
            ostage[g, :, :, lanes] = attended.astype(ostage.dtype).reshape(2, tokens, DH)
        out_home(g).start()
        out_away(g).start()
        return 0

    lax.fori_loop(0, chunks, attend, 0)

    send_mask().wait_send()

    def drain(g, _):
        send_q(g).wait_send()
        for kv in range(2):
            to_sibling(kv, g).wait_send()
        for i in range(nr - 1):
            def body(i=i):
                for core in range(2):
                    for kv in range(2):
                        to_row(kv, i, g, core).wait_send()
            guard(row_ok(i), body)
        for i in range(2):
            def body(i=i):
                for kv in range(2):
                    for core in range(2):
                        to_frame(kv, i, g, core).wait_send()
                    for j in range(nr - 1):
                        def inner(j=j, kv=kv):
                            forward(kv, j, i, g).wait_send()
                        guard(row_ok(j), inner)
            guard(frames[i][1], body)
        out_home(g).wait()
        out_away(g).wait_send()
        out_arrived(g).wait_recv()
        return 0

    lax.fori_loop(0, chunks, drain, 0)


def solution(mesh):
    n_tm, n_height = mesh.shape["tm"], mesh.shape["height"]

    def per_device(queries, keys, values, windows, tile_mask, coefficient, layer, steering):
        frames, rows, cols, tile, features = queries.shape
        heads = features // DH
        tokens = frames * rows * cols * tile
        chunks = heads // 2 // HC
        cw = HC * DH
        span = 2 * tokens
        nr = min(n_height, 3)
        ns = 3 * nr
        flat = (tokens, features)
        hbm = pl.BlockSpec(memory_space=pl.ANY)
        vmem = pl.BlockSpec(memory_space=pltpu.VMEM)
        smem = pl.BlockSpec(memory_space=pltpu.SMEM)
        bf16 = jnp.bfloat16
        out = pl.pallas_call(
            functools.partial(kernel, n_tm, n_height, heads),
            out_shape=jax.ShapeDtypeStruct(flat, bf16),
            in_specs=[hbm, hbm, hbm, smem, vmem, smem, smem, vmem],
            out_specs=hbm,
            scratch_shapes=[
                pltpu.VMEM((ns, chunks, 2, tokens, cw), bf16),
                pltpu.VMEM((ns, chunks, 2, tokens, cw), bf16),
                pltpu.VMEM((chunks, 2, tokens, cw), bf16),
                pltpu.VMEM((cols, tile_mask.shape[-1]), jnp.int32),
                pltpu.VMEM((2 * ns + 1, span, span), jnp.float32),
                pltpu.VMEM((ns, span, span), jnp.float32),
                pltpu.VMEM((heads, 1, DH), jnp.float32),
                pltpu.VMEM((chunks, 2, tokens, cw), bf16),
                pltpu.SemaphoreType.DMA((2, 3 * nr, chunks, 2)),
                pltpu.SemaphoreType.DMA((2, ns, chunks, 2)),
                pltpu.SemaphoreType.DMA((4, chunks)),
                pltpu.SemaphoreType.DMA((2, chunks)),
                pltpu.SemaphoreType.DMA((2,)),
                pltpu.SemaphoreType.DMA((2, chunks)),
            ],
            compiler_params=pltpu.CompilerParams(
                collective_id=0, has_side_effects=True, vmem_limit_bytes=48 * 1024 * 1024
            ),
        )(
            queries.reshape(flat), keys.reshape(flat), values.reshape(flat), windows,
            tile_mask.reshape(cols, tile_mask.shape[-1]), coefficient, layer, steering,
        )
        return out.reshape(queries.shape)

    tiles = P(("sweep", "tm"), "height", "width", None, None)
    return jax.shard_map(
        per_device,
        mesh=mesh,
        in_specs=(tiles, tiles, tiles, P(), P("tm", "height", "width", None), P("sweep"), P("sweep"), P()),
        out_specs=tiles,
        check_vma=False,
    )
```

```python
import functools
import math

import jax
import jax.numpy as jnp
from jax import lax
from jax.experimental import pallas as pl
from jax.experimental.pallas import tpu as pltpu
from jax.sharding import PartitionSpec as P

DH = 128
NEG = -1e30
MESH = pl.DeviceIdType.MESH
HC = 2


def kernel(
    n_tm, n_height, heads, reach_chunks,
    q_hbm, k_hbm, v_hbm, win_ref, mask_hbm, coef_ref, layer_ref, steer_hbm,
    out_ref,
    kbuf, vbuf, qbuf, mbuf, bias, scores, svec, ostage,
    raw, byhead, q_ref, k_ref, v_ref, owhole, mask_ref, steer_ref, rank, perm,
    ssem, rsem, lsem, qsem, msem, osem, isem,
):
    tokens = raw.shape[1]
    cols = mask_ref.shape[0]
    tile = tokens // cols
    all_cols = 2 * cols
    half = (heads // 2) * DH
    cw = HC * DH
    chunks = half // cw
    c = lax.axis_index("width")
    z = lax.axis_index("tm")
    x = lax.axis_index("height")
    sib = 1 - c
    if n_height == 1:
        rows = []
    elif n_height == 2:
        rows = [(1 - 2 * x, True, 1)]
    else:
        rows = [(-1, x > 0, 2), (1, x < n_height - 1, 1)]
    nr = 1 + len(rows)
    ns = 3 * nr
    frames = [(-1, z > 0, 2), (1, z < n_tm - 1, 1)]
    bufs = ((k_ref, kbuf), (v_ref, vbuf))

    def guard(cond, body):
        if cond is True:
            body()
        else:
            pl.when(cond)(body)

    loads = [
        pltpu.make_async_copy(src, raw.at[i], isem.at[i])
        for i, src in enumerate((k_hbm, v_hbm, q_hbm))
    ]
    loads.append(pltpu.make_async_copy(mask_hbm, mask_ref, isem.at[3]))
    loads.append(pltpu.make_async_copy(steer_hbm, steer_ref, isem.at[4]))
    for load in loads:
        load.start()

    barrier = pltpu.get_barrier_semaphore()

    def greet(**where):
        pl.semaphore_signal(barrier, inc=1, device_id=where, device_id_type=MESH)

    greet(width=sib)
    expect = jnp.int32(1)
    for d, ok, _ in rows:
        def body(d=d):
            for t in range(2):
                greet(height=x + d, width=jnp.int32(t))
        guard(ok, body)
        expect = expect + (2 if ok is True else 2 * ok.astype(jnp.int32))
    for d, ok, _ in frames:
        def body(d=d):
            for t in range(2):
                greet(tm=z + d, width=jnp.int32(t))
        guard(ok, body)
        expect = expect + 2 * ok.astype(jnp.int32)

    reaching = jnp.int32(0)
    flags = [jnp.where(win_ref[0, h] >= 1, 1, 0) for h in range(heads)]
    for h in range(heads):
        rank[h] = reaching
        reaching = reaching + flags[h]
    for h in range(heads):
        rank[h] = jnp.where(flags[h] == 1, rank[h], reaching + h - rank[h])

    def invert(i, _):
        head = jnp.int32(0)
        for h in range(heads):
            head = jnp.where(rank[h] == i, h, head)
        perm[i] = head
        return 0

    lax.fori_loop(0, heads, invert, 0)

    def pack(which, ref):
        loads[which].wait()
        for h in range(heads):
            byhead[which, h] = raw[which, :, h * DH : (h + 1) * DH]

        def one(g, _):
            for core in range(2):
                for hh in range(HC):
                    head = perm[(g * HC + hh) * 2 + core]
                    ref[g, core, :, hh * DH : (hh + 1) * DH] = byhead[which, head]
            return 0

        lax.fori_loop(0, chunks, one, 0)

    pack(0, k_ref)
    pack(1, v_ref)
    pl.semaphore_wait(barrier, expect)

    def remote(src, dst, s, r, where):
        return pltpu.make_async_remote_copy(
            src_ref=src, dst_ref=dst, send_sem=s, recv_sem=r, device_id=where, device_id_type=MESH
        )

    def own(kv, dest, g, core, slot, where):
        src, buf = bufs[kv]
        return remote(
            src.at[g, core], buf.at[slot, g, c],
            ssem.at[kv, dest, g, core], rsem.at[kv, slot, g, c], where,
        )

    def to_sibling(kv, g):
        return own(kv, 0, g, sib, 0, dict(width=sib))

    def to_row(kv, i, g, core):
        d, _, there = rows[i]
        return own(kv, 1 + i, g, jnp.int32(core), there, dict(height=x + d, width=jnp.int32(core)))

    def to_frame(kv, i, g, core):
        d, _, there = frames[i]
        return own(kv, nr + i, g, jnp.int32(core), there * nr, dict(tm=z + d, width=jnp.int32(core)))

    def forward(kv, j, i, g):
        d, _, there = frames[i]
        buf = bufs[kv][1]
        return remote(
            buf.at[1 + j, g], buf.at[there * nr + 1 + j, g],
            ssem.at[kv, nr + 2 + 2 * j + i, g, 0], rsem.at[kv, there * nr + 1 + j, g, 0],
            dict(tm=z + d),
        )

    def arrived(kv, slot, g, core):
        src, buf = bufs[kv]
        return remote(
            src.at[g, core], buf.at[slot, g, core],
            ssem.at[kv, 0, g, core], rsem.at[kv, slot, g, core], dict(width=sib),
        )

    def forwarded(kv, slot, g):
        buf = bufs[kv][1]
        return remote(
            buf.at[slot, g], buf.at[slot, g],
            ssem.at[kv, 0, g, 0], rsem.at[kv, slot, g, 0], dict(width=sib),
        )

    def keep(kv, g):
        src, buf = bufs[kv]
        return pltpu.make_async_copy(src.at[g, c], buf.at[0, g, c], lsem.at[kv, g])

    def keep_q(g):
        return pltpu.make_async_copy(q_ref.at[g, c], qbuf.at[g, c], lsem.at[2, g])

    def send_q(g):
        return remote(
            q_ref.at[g, sib], qbuf.at[g, c], qsem.at[0, g], qsem.at[1, g], dict(width=sib)
        )

    def send_mask():
        return remote(mask_hbm, mbuf, msem.at[0], msem.at[1], dict(width=sib))

    def row_ok(i):
        return rows[i][1]

    send_mask().start()

    def start_rows(g, _):
        for i in range(nr - 1):
            def body(i=i):
                for core in range(2):
                    for kv in range(2):
                        to_row(kv, i, g, core).start()
            guard(row_ok(i), body)
        return 0

    def start_frames(g):
        for i in range(2):
            def body(i=i):
                for core in range(2):
                    for kv in range(2):
                        to_frame(kv, i, g, core).start()
            guard(frames[i][1], body)

    def start_local(g, _):
        keep_q(g).start()
        send_q(g).start()
        for kv in range(2):
            keep(kv, g).start()
            to_sibling(kv, g).start()
        return 0

    start_rows(0, 0)
    start_frames(0)
    lax.fori_loop(1, chunks, start_rows, 0)
    pack(2, q_ref)
    lax.fori_loop(0, chunks, start_local, 0)
    loads[3].wait()
    loads[4].wait()

    for i in range(nr - 1):
        if row_ok(i) is not True:
            @pl.when(jnp.logical_not(row_ok(i)))
            def _(i=i):
                for f in range(3):
                    for _, buf in bufs:
                        buf[f * nr + 1 + i] = jnp.zeros(buf.shape[1:], buf.dtype)
    for i in range(2):
        @pl.when(jnp.logical_not(frames[i][1]))
        def _(i=i):
            for j in range(nr):
                for _, buf in bufs:
                    def zero(g, _, j=j, buf=buf):
                        buf[(1 + i) * nr + j, g] = jnp.zeros(buf.shape[2:], buf.dtype)
                        return 0
                    if j == 0 or row_ok(j - 1) is True:
                        lax.fori_loop(0, reach_chunks, zero, 0)
                    else:
                        @pl.when(row_ok(j - 1))
                        def _(zero=zero):
                            lax.fori_loop(0, reach_chunks, zero, 0)

    pick = lax.broadcasted_iota(jnp.int32, (steer_ref.shape[0], DH), 0) == layer_ref[0]
    for h in range(heads):
        rows_f32 = steer_ref[:, h * DH : (h + 1) * DH].astype(jnp.float32)
        svec[h] = coef_ref[0] * jnp.sum(jnp.where(pick, rows_f32, 0.0), axis=0, keepdims=True)

    def pump(g, _):
        @pl.when(g > 0)
        def _():
            start_frames(g)
        for j in range(nr - 1):
            def body(j=j):
                for core in range(2):
                    for kv in range(2):
                        arrived(kv, 1 + j, g, jnp.int32(core)).wait_recv()
                for i in range(2):
                    def inner(i=i):
                        for kv in range(2):
                            forward(kv, j, i, g).start()
                    guard(frames[i][1], inner)
            guard(row_ok(j), body)
        return 0

    lax.fori_loop(0, reach_chunks, pump, 0)

    send_mask().wait_recv()
    theirs = mbuf[...]
    mine = mask_ref[...]
    first = jnp.where(c == 0, mine, theirs)
    second = jnp.where(c == 0, theirs, mine)
    kept = jnp.concatenate([first, second], axis=0)
    span = all_cols * tile
    lane = lax.broadcasted_iota(jnp.int32, (1, kept.shape[1]), 1)
    block = lax.broadcasted_iota(jnp.int32, (1, span), 1) // tile
    for f in range(3):
        df = (0, -1, 1)[f]
        f_ok = True if f == 0 else frames[f - 1][1]
        for r in range(nr):
            dr = 0 if r == 0 else rows[r - 1][0]
            r_ok = True if r == 0 else row_ok(r - 1)
            base = 9 * (df + 1) + 3 * (dr + 1)
            slot = f * nr + r
            ok = None
            for cond in (f_ok, r_ok):
                if cond is not True:
                    ok = cond if ok is None else jnp.logical_and(ok, cond)
            for qc in range(all_cols):
                line = jnp.full((1, span), NEG, jnp.float32)
                for kc in range(max(qc - 1, 0), min(qc + 2, all_cols)):
                    if slot == 0 and kc == qc:
                        value = jnp.zeros((1, 1), jnp.float32)
                    else:
                        here = jnp.where(lane == base + (kc - qc + 1), kept[qc : qc + 1], 0)
                        hit = jnp.sum(here.astype(jnp.float32), axis=1, keepdims=True)
                        value = jnp.where(hit == 1.0, 0.0, NEG)
                        if ok is not None:
                            value = jnp.where(ok, value, NEG)
                    line = jnp.where(block == kc, value, line)
                alone = jnp.where(block == qc, line, NEG)
                at = pl.ds(qc * tile, tile)
                bias[slot, at, :] = jnp.broadcast_to(alone, (tile, span))
                bias[ns + slot, at, :] = jnp.broadcast_to(line, (tile, span))
    bias[2 * ns] = jnp.full((span, span), NEG, jnp.float32)

    scale = 1.0 / math.sqrt(DH)

    def place(core, g):
        return owhole.at[core, pl.ds(g * HC, HC)]

    def out_home(g):
        return pltpu.make_async_copy(ostage.at[g, c], place(c, g), lsem.at[3, g])

    def out_away(g):
        return remote(
            ostage.at[g, sib], place(c, g), osem.at[0, g], osem.at[1, g], dict(width=sib)
        )

    def out_arrived(g):
        return remote(
            ostage.at[g, sib], place(sib, g), osem.at[0, g], osem.at[1, g], dict(width=sib)
        )

    def attend(far, g, _):
        keep_q(g).wait()
        send_q(g).wait_recv()
        for kv in range(2):
            keep(kv, g).wait()
            arrived(kv, 0, g, sib).wait_recv()
        if not far:
            for j in range(nr - 1):
                def near(j=j):
                    for core in range(2):
                        for kv in range(2):
                            arrived(kv, 1 + j, g, jnp.int32(core)).wait_recv()
                guard(row_ok(j), near)
        for i in range(2 if far else 0):
            def body(i=i):
                for kv in range(2):
                    for core in range(2):
                        arrived(kv, (1 + i) * nr, g, jnp.int32(core)).wait_recv()
                    for j in range(nr - 1):
                        def inner(j=j, kv=kv):
                            forwarded(kv, (1 + i) * nr + 1 + j, g).wait_recv()
                        guard(row_ok(j), inner)
            guard(frames[i][1], body)
        for hh in range(HC):
            h = perm[(g * HC + hh) * 2 + c]
            lanes = slice(hh * DH, (hh + 1) * DH)
            wf, wr, wc = win_ref[0, h], win_ref[1, h], win_ref[2, h]
            q = qbuf[g][:, :, lanes].reshape(span, DH)
            top = None
            for slot in range(ns if far else nr):
                index = jnp.where(wc >= 1, ns + slot, slot)
                if slot // nr > 0:
                    index = jnp.where(wf >= 1, index, 2 * ns)
                if slot % nr > 0:
                    index = jnp.where(wr >= 1, index, 2 * ns)
                key = kbuf[slot, g][:, :, lanes].reshape(span, DH)
                s = lax.dot_general(
                    q, key, (((1,), (1,)), ((), ())), preferred_element_type=jnp.float32
                )
                s = s * scale + bias[index]
                scores[slot] = s
                high = jnp.maximum(s[:, :DH], s[:, DH:]) if span == 2 * DH else jnp.max(s, axis=1, keepdims=True)
                top = high if top is None else jnp.maximum(top, high)
            top = jnp.max(top, axis=1, keepdims=True)
            total = None
            mixture = None
            for slot in range(ns if far else nr):
                e = jnp.exp(scores[slot] - top)
                part = e[:, :DH] + e[:, DH:] if span == 2 * DH else jnp.sum(e, axis=1, keepdims=True)
                total = part if total is None else total + part
                value = vbuf[slot, g][:, :, lanes].reshape(span, DH)
                term = jnp.dot(e.astype(jnp.bfloat16), value, preferred_element_type=jnp.float32)
                mixture = term if mixture is None else mixture + term
            total = jnp.sum(total, axis=1, keepdims=True)
            attended = mixture * (1.0 / total) + svec[h]
            attended = attended.astype(ostage.dtype)
            ostage[g, 0, hh] = attended[:tokens]
            ostage[g, 1, hh] = attended[tokens:]
        out_home(g).start()
        out_away(g).start()
        return 0

    last = reach_chunks - 1
    lax.fori_loop(0, last, functools.partial(attend, True), 0)
    if reach_chunks < chunks:
        lax.fori_loop(reach_chunks, chunks, functools.partial(attend, False), 0)
    lax.fori_loop(last, reach_chunks, functools.partial(attend, True), 0)

    send_mask().wait_send()

    def drain(far, g, _):
        send_q(g).wait_send()
        for kv in range(2):
            to_sibling(kv, g).wait_send()
        for i in range(nr - 1):
            def body(i=i):
                for core in range(2):
                    for kv in range(2):
                        to_row(kv, i, g, core).wait_send()
            guard(row_ok(i), body)
        for i in range(2 if far else 0):
            def body(i=i):
                for kv in range(2):
                    for core in range(2):
                        to_frame(kv, i, g, core).wait_send()
                    for j in range(nr - 1):
                        def inner(j=j, kv=kv):
                            forward(kv, j, i, g).wait_send()
                        guard(row_ok(j), inner)
            guard(frames[i][1], body)
        out_home(g).wait()
        out_away(g).wait_send()
        out_arrived(g).wait_recv()
        return 0

    lax.fori_loop(0, reach_chunks, functools.partial(drain, True), 0)
    if reach_chunks < chunks:
        lax.fori_loop(reach_chunks, chunks, functools.partial(drain, False), 0)

    for h in range(heads):
        spot = rank[h]
        out_ref[:, h * DH : (h + 1) * DH] = owhole[spot & 1, spot >> 1]


def solution(mesh):
    n_tm, n_height = mesh.shape["tm"], mesh.shape["height"]

    def per_device(queries, keys, values, windows, tile_mask, coefficient, layer, steering):
        frames, rows, cols, tile, features = queries.shape
        heads = features // DH
        tokens = frames * rows * cols * tile
        chunks = heads // 2 // HC
        cw = HC * DH
        span = 2 * tokens
        nr = min(n_height, 3)
        ns = 3 * nr
        flat = (tokens, features)
        hbm = pl.BlockSpec(memory_space=pltpu.MemorySpace.HBM)
        vmem = pl.BlockSpec(memory_space=pltpu.VMEM)
        smem = pl.BlockSpec(memory_space=pltpu.SMEM)
        bf16 = jnp.bfloat16
        offsets = tile_mask.shape[-1]
        packed = pltpu.VMEM((chunks, 2, tokens, cw), bf16)

        def attention(number, reach_chunks):
            return pl.pallas_call(
                functools.partial(kernel, n_tm, n_height, heads, reach_chunks),
                out_shape=jax.ShapeDtypeStruct(flat, bf16),
                in_specs=[hbm, hbm, hbm, smem, hbm, smem, smem, hbm],
                out_specs=vmem,
                scratch_shapes=[
                    pltpu.VMEM((ns, chunks, 2, tokens, cw), bf16),
                    pltpu.VMEM((ns, chunks, 2, tokens, cw), bf16),
                    packed,
                    pltpu.VMEM((cols, offsets), jnp.int32),
                    pltpu.VMEM((2 * ns + 1, span, span), jnp.float32),
                    pltpu.VMEM((ns, span, span), jnp.float32),
                    pltpu.VMEM((heads, 1, DH), jnp.float32),
                    pltpu.VMEM((chunks, 2, HC, tokens, DH), bf16),
                    pltpu.VMEM((3, tokens, features), bf16),
                    pltpu.VMEM((3, heads, tokens, DH), bf16),
                    packed,
                    packed,
                    packed,
                    pltpu.VMEM((2, chunks * HC, tokens, DH), bf16),
                    pltpu.VMEM((cols, offsets), jnp.int32),
                    pltpu.VMEM(steering.shape, bf16),
                    pltpu.SMEM((heads,), jnp.int32),
                    pltpu.SMEM((heads,), jnp.int32),
                    pltpu.SemaphoreType.DMA((2, 3 * nr, chunks, 2)),
                    pltpu.SemaphoreType.DMA((2, ns, chunks, 2)),
                    pltpu.SemaphoreType.DMA((4, chunks)),
                    pltpu.SemaphoreType.DMA((2, chunks)),
                    pltpu.SemaphoreType.DMA((2,)),
                    pltpu.SemaphoreType.DMA((2, chunks)),
                    pltpu.SemaphoreType.DMA((5,)),
                ],
                compiler_params=pltpu.CompilerParams(
                    collective_id=number, has_side_effects=True, vmem_limit_bytes=48 * 1024 * 1024
                ),
            )

        least = 2
        reaching = jnp.sum((windows[:, 0] >= 1).astype(jnp.int32))
        needed = sum((reaching > 2 * HC * n).astype(jnp.int32) for n in range(least, chunks))
        out = lax.switch(
            needed,
            [attention(n, least + n) for n in range(chunks - least + 1)],
            queries.reshape(flat), keys.reshape(flat), values.reshape(flat), windows.T,
            tile_mask.reshape(cols, offsets), coefficient, layer, steering,
        )
        return out.reshape(queries.shape)

    tiles = P(("sweep", "tm"), "height", "width", None, None)
    return jax.shard_map(
        per_device,
        mesh=mesh,
        in_specs=(tiles, tiles, tiles, P(), P("tm", "height", "width", None), P("sweep"), P("sweep"), P()),
        out_specs=tiles,
        check_vma=False,
    )
```

```python
import functools
import math

import jax
import jax.numpy as jnp
from jax import lax
from jax.experimental import pallas as pl
from jax.experimental.pallas import tpu as pltpu
from jax.sharding import PartitionSpec as P

DH = 128
NEG = -1e30
MESH = pl.DeviceIdType.MESH
HC = 1
FULL, CROSS, NEAR = range(3)


def kernel(
    n_tm, n_height, heads, full_chunks, reach_chunks,
    q_hbm, k_hbm, v_hbm, win_ref, mask_hbm, coef_ref, layer_ref, steer_hbm,
    out_ref,
    kbuf, vbuf, qbuf, mbuf, bias, scores, svec, ostage,
    raw, byhead, q_ref, k_ref, v_ref, owhole, mask_ref, steer_ref, rank, perm,
    ssem, rsem, lsem, qsem, msem, osem, isem,
):
    tokens = raw.shape[1]
    cols = mask_ref.shape[0]
    tile = tokens // cols
    all_cols = 2 * cols
    half = (heads // 2) * DH
    cw = HC * DH
    chunks = half // cw
    c = lax.axis_index("width")
    z = lax.axis_index("tm")
    x = lax.axis_index("height")
    sib = 1 - c
    if n_height == 1:
        rows = []
    elif n_height == 2:
        rows = [(1 - 2 * x, True, 1)]
    else:
        rows = [(-1, x > 0, 2), (1, x < n_height - 1, 1)]
    nr = 1 + len(rows)
    ns = 3 * nr
    frames = [(-1, z > 0, 2), (1, z < n_tm - 1, 1)]
    bufs = ((k_ref, kbuf), (v_ref, vbuf))

    def guard(cond, body):
        if cond is True:
            body()
        else:
            pl.when(cond)(body)

    loads = [
        pltpu.make_async_copy(src, raw.at[i], isem.at[i])
        for i, src in enumerate((k_hbm, v_hbm, q_hbm))
    ]
    loads.append(pltpu.make_async_copy(mask_hbm, mask_ref, isem.at[3]))
    loads.append(pltpu.make_async_copy(steer_hbm, steer_ref, isem.at[4]))
    for load in loads:
        load.start()

    barrier = pltpu.get_barrier_semaphore()

    def greet(**where):
        pl.semaphore_signal(barrier, inc=1, device_id=where, device_id_type=MESH)

    greet(width=sib)
    expect = jnp.int32(1)
    for d, ok, _ in rows:
        def body(d=d):
            for t in range(2):
                greet(height=x + d, width=jnp.int32(t))
        guard(ok, body)
        expect = expect + (2 if ok is True else 2 * ok.astype(jnp.int32))
    for d, ok, _ in frames:
        def body(d=d):
            for t in range(2):
                greet(tm=z + d, width=jnp.int32(t))
        guard(ok, body)
        expect = expect + 2 * ok.astype(jnp.int32)

    along = [jnp.where(win_ref[0, h] >= 1, 1, 0) for h in range(heads)]
    both = [along[h] * jnp.where(win_ref[1, h] >= 1, 1, 0) for h in range(heads)]
    n_along = functools.reduce(lambda a, b: a + b, along)
    n_both = functools.reduce(lambda a, b: a + b, both)
    place_both, place_along, place_rest = jnp.int32(0), n_both, n_along
    for h in range(heads):
        rank[h] = jnp.where(
            both[h] == 1, place_both, jnp.where(along[h] == 1, place_along, place_rest)
        )
        place_both = place_both + both[h]
        place_along = place_along + along[h] - both[h]
        place_rest = place_rest + 1 - along[h]

    def invert(i, _):
        head = jnp.int32(0)
        for h in range(heads):
            head = jnp.where(rank[h] == i, h, head)
        perm[i] = head
        return 0

    lax.fori_loop(0, heads, invert, 0)

    def pack(which, ref):
        loads[which].wait()
        for h in range(heads):
            byhead[which, h] = raw[which, :, h * DH : (h + 1) * DH]

        def one(g, _):
            for core in range(2):
                for hh in range(HC):
                    head = perm[(g * HC + hh) * 2 + core]
                    ref[g, core, :, hh * DH : (hh + 1) * DH] = byhead[which, head]
            return 0

        lax.fori_loop(0, chunks, one, 0)

    pack(0, k_ref)
    pack(1, v_ref)
    pl.semaphore_wait(barrier, expect)

    def remote(src, dst, s, r, where):
        return pltpu.make_async_remote_copy(
            src_ref=src, dst_ref=dst, send_sem=s, recv_sem=r, device_id=where, device_id_type=MESH
        )

    def own(kv, dest, g, core, slot, where):
        src, buf = bufs[kv]
        return remote(
            src.at[g, core], buf.at[slot, g, c],
            ssem.at[kv, dest, g, core], rsem.at[kv, slot, g, c], where,
        )

    def to_sibling(kv, g):
        return own(kv, 0, g, sib, 0, dict(width=sib))

    def to_row(kv, i, g, core):
        d, _, there = rows[i]
        return own(kv, 1 + i, g, jnp.int32(core), there, dict(height=x + d, width=jnp.int32(core)))

    def to_frame(kv, i, g, core):
        d, _, there = frames[i]
        return own(kv, nr + i, g, jnp.int32(core), there * nr, dict(tm=z + d, width=jnp.int32(core)))

    def forward(kv, j, i, g):
        d, _, there = frames[i]
        buf = bufs[kv][1]
        return remote(
            buf.at[1 + j, g], buf.at[there * nr + 1 + j, g],
            ssem.at[kv, nr + 2 + 2 * j + i, g, 0], rsem.at[kv, there * nr + 1 + j, g, 0],
            dict(tm=z + d),
        )

    def arrived(kv, slot, g, core):
        src, buf = bufs[kv]
        return remote(
            src.at[g, core], buf.at[slot, g, core],
            ssem.at[kv, 0, g, core], rsem.at[kv, slot, g, core], dict(width=sib),
        )

    def forwarded(kv, slot, g):
        buf = bufs[kv][1]
        return remote(
            buf.at[slot, g], buf.at[slot, g],
            ssem.at[kv, 0, g, 0], rsem.at[kv, slot, g, 0], dict(width=sib),
        )

    def keep(kv, g):
        src, buf = bufs[kv]
        return pltpu.make_async_copy(src.at[g, c], buf.at[0, g, c], lsem.at[kv, g])

    def keep_q(g):
        return pltpu.make_async_copy(q_ref.at[g, c], qbuf.at[g, c], lsem.at[2, g])

    def send_q(g):
        return remote(
            q_ref.at[g, sib], qbuf.at[g, c], qsem.at[0, g], qsem.at[1, g], dict(width=sib)
        )

    def send_mask():
        return remote(mask_hbm, mbuf, msem.at[0], msem.at[1], dict(width=sib))

    def row_ok(i):
        return rows[i][1]

    send_mask().start()

    def start_rows(g, _):
        for i in range(nr - 1):
            def body(i=i):
                for core in range(2):
                    for kv in range(2):
                        to_row(kv, i, g, core).start()
            guard(row_ok(i), body)
        return 0

    def start_frames(g):
        for i in range(2):
            def body(i=i):
                for core in range(2):
                    for kv in range(2):
                        to_frame(kv, i, g, core).start()
            guard(frames[i][1], body)

    def start_local(g, _):
        keep_q(g).start()
        send_q(g).start()
        for kv in range(2):
            keep(kv, g).start()
            to_sibling(kv, g).start()
        return 0

    start_rows(0, 0)
    start_frames(0)
    lax.fori_loop(1, chunks, start_rows, 0)
    pack(2, q_ref)
    lax.fori_loop(0, chunks, start_local, 0)
    loads[3].wait()
    loads[4].wait()

    for i in range(nr - 1):
        if row_ok(i) is not True:
            @pl.when(jnp.logical_not(row_ok(i)))
            def _(i=i):
                for f in range(3):
                    for _, buf in bufs:
                        buf[f * nr + 1 + i] = jnp.zeros(buf.shape[1:], buf.dtype)
    for i in range(2):
        @pl.when(jnp.logical_not(frames[i][1]))
        def _(i=i):
            for j in range(nr):
                for _, buf in bufs:
                    def zero(g, _, j=j, buf=buf):
                        buf[(1 + i) * nr + j, g] = jnp.zeros(buf.shape[2:], buf.dtype)
                        return 0
                    count = reach_chunks if j == 0 else full_chunks
                    if j == 0 or row_ok(j - 1) is True:
                        lax.fori_loop(0, count, zero, 0)
                    else:
                        @pl.when(row_ok(j - 1))
                        def _(zero=zero, count=count):
                            lax.fori_loop(0, count, zero, 0)

    pick = lax.broadcasted_iota(jnp.int32, (steer_ref.shape[0], DH), 0) == layer_ref[0]
    for h in range(heads):
        rows_f32 = steer_ref[:, h * DH : (h + 1) * DH].astype(jnp.float32)
        svec[h] = coef_ref[0] * jnp.sum(jnp.where(pick, rows_f32, 0.0), axis=0, keepdims=True)

    def pump(g, _):
        @pl.when(g > 0)
        def _():
            start_frames(g)
        for j in range(nr - 1):
            def body(j=j):
                for core in range(2):
                    for kv in range(2):
                        arrived(kv, 1 + j, g, jnp.int32(core)).wait_recv()
                for i in range(2):
                    def inner(i=i):
                        for kv in range(2):
                            forward(kv, j, i, g).start()
                    guard(frames[i][1], inner)
            guard(row_ok(j), body)
        return 0

    lax.fori_loop(0, full_chunks, pump, 0)

    def straight(g, _):
        start_frames(g)
        return 0

    if full_chunks < reach_chunks:
        lax.fori_loop(full_chunks, reach_chunks, straight, 0)

    send_mask().wait_recv()
    theirs = mbuf[...]
    mine = mask_ref[...]
    first = jnp.where(c == 0, mine, theirs)
    second = jnp.where(c == 0, theirs, mine)
    kept = jnp.concatenate([first, second], axis=0)
    span = all_cols * tile
    lane = lax.broadcasted_iota(jnp.int32, (1, kept.shape[1]), 1)
    block = lax.broadcasted_iota(jnp.int32, (1, span), 1) // tile
    for f in range(3):
        df = (0, -1, 1)[f]
        f_ok = True if f == 0 else frames[f - 1][1]
        for r in range(nr):
            dr = 0 if r == 0 else rows[r - 1][0]
            r_ok = True if r == 0 else row_ok(r - 1)
            base = 9 * (df + 1) + 3 * (dr + 1)
            slot = f * nr + r
            ok = None
            for cond in (f_ok, r_ok):
                if cond is not True:
                    ok = cond if ok is None else jnp.logical_and(ok, cond)
            for qc in range(all_cols):
                line = jnp.full((1, span), NEG, jnp.float32)
                for kc in range(max(qc - 1, 0), min(qc + 2, all_cols)):
                    if slot == 0 and kc == qc:
                        value = jnp.zeros((1, 1), jnp.float32)
                    else:
                        here = jnp.where(lane == base + (kc - qc + 1), kept[qc : qc + 1], 0)
                        hit = jnp.sum(here.astype(jnp.float32), axis=1, keepdims=True)
                        value = jnp.where(hit == 1.0, 0.0, NEG)
                        if ok is not None:
                            value = jnp.where(ok, value, NEG)
                    line = jnp.where(block == kc, value, line)
                alone = jnp.where(block == qc, line, NEG)
                at = pl.ds(qc * tile, tile)
                bias[slot, at, :] = jnp.broadcast_to(alone, (tile, span))
                bias[ns + slot, at, :] = jnp.broadcast_to(line, (tile, span))
    bias[2 * ns] = jnp.full((span, span), NEG, jnp.float32)

    scale = 1.0 / math.sqrt(DH)

    def place(core, g):
        return owhole.at[core, pl.ds(g * HC, HC)]

    def out_home(g):
        return pltpu.make_async_copy(ostage.at[g, c], place(c, g), lsem.at[3, g])

    def out_away(g):
        return remote(
            ostage.at[g, sib], place(c, g), osem.at[0, g], osem.at[1, g], dict(width=sib)
        )

    def out_arrived(g):
        return remote(
            ostage.at[g, sib], place(sib, g), osem.at[0, g], osem.at[1, g], dict(width=sib)
        )

    def attend(kind, g, _):
        slots = [
            slot for slot in range(ns)
            if kind == FULL or slot < nr or (kind == CROSS and slot % nr == 0)
        ]
        keep_q(g).wait()
        send_q(g).wait_recv()
        for kv in range(2):
            keep(kv, g).wait()
            arrived(kv, 0, g, sib).wait_recv()
        if kind != FULL:
            for j in range(nr - 1):
                def near(j=j):
                    for core in range(2):
                        for kv in range(2):
                            arrived(kv, 1 + j, g, jnp.int32(core)).wait_recv()
                guard(row_ok(j), near)
        for i in range(2 if kind != NEAR else 0):
            def body(i=i):
                for kv in range(2):
                    for core in range(2):
                        arrived(kv, (1 + i) * nr, g, jnp.int32(core)).wait_recv()
                    for j in range(nr - 1 if kind == FULL else 0):
                        def inner(j=j, kv=kv):
                            forwarded(kv, (1 + i) * nr + 1 + j, g).wait_recv()
                        guard(row_ok(j), inner)
            guard(frames[i][1], body)
        for hh in range(HC):
            h = perm[(g * HC + hh) * 2 + c]
            lanes = slice(hh * DH, (hh + 1) * DH)
            wf, wr, wc = win_ref[0, h], win_ref[1, h], win_ref[2, h]
            q = qbuf[g][:, :, lanes].reshape(span, DH)
            top = None
            for slot in slots:
                index = jnp.where(wc >= 1, ns + slot, slot)
                if slot // nr > 0:
                    index = jnp.where(wf >= 1, index, 2 * ns)
                if slot % nr > 0:
                    index = jnp.where(wr >= 1, index, 2 * ns)
                key = kbuf[slot, g][:, :, lanes].reshape(span, DH)
                s = lax.dot_general(
                    q, key, (((1,), (1,)), ((), ())), preferred_element_type=jnp.float32
                )
                s = s * scale + bias[index]
                scores[slot] = s
                high = jnp.maximum(s[:, :DH], s[:, DH:]) if span == 2 * DH else jnp.max(s, axis=1, keepdims=True)
                top = high if top is None else jnp.maximum(top, high)
            top = jnp.max(top, axis=1, keepdims=True)
            total = None
            mixture = None
            for slot in slots:
                e = jnp.exp(scores[slot] - top)
                part = e[:, :DH] + e[:, DH:] if span == 2 * DH else jnp.sum(e, axis=1, keepdims=True)
                total = part if total is None else total + part
                value = vbuf[slot, g][:, :, lanes].reshape(span, DH)
                term = jnp.dot(e.astype(jnp.bfloat16), value, preferred_element_type=jnp.float32)
                mixture = term if mixture is None else mixture + term
            total = jnp.sum(total, axis=1, keepdims=True)
            attended = mixture * (1.0 / total) + svec[h]
            attended = attended.astype(ostage.dtype)
            ostage[g, 0, hh] = attended[:tokens]
            ostage[g, 1, hh] = attended[tokens:]
        out_home(g).start()
        out_away(g).start()
        return 0

    def run(start, stop, step, kind):
        if start < stop:
            lax.fori_loop(start, stop, functools.partial(step, kind), 0)

    if full_chunks == reach_chunks and 2 * full_chunks > chunks:
        run(reach_chunks, chunks, attend, NEAR)
        run(0, full_chunks, attend, FULL)
    else:
        run(0, full_chunks, attend, FULL)
        run(reach_chunks, chunks, attend, NEAR)
        run(full_chunks, reach_chunks, attend, CROSS)

    send_mask().wait_send()

    def drain(kind, g, _):
        send_q(g).wait_send()
        for kv in range(2):
            to_sibling(kv, g).wait_send()
        for i in range(nr - 1):
            def body(i=i):
                for core in range(2):
                    for kv in range(2):
                        to_row(kv, i, g, core).wait_send()
            guard(row_ok(i), body)
        for i in range(2 if kind != NEAR else 0):
            def body(i=i):
                for kv in range(2):
                    for core in range(2):
                        to_frame(kv, i, g, core).wait_send()
                    for j in range(nr - 1 if kind == FULL else 0):
                        def inner(j=j, kv=kv):
                            forward(kv, j, i, g).wait_send()
                        guard(row_ok(j), inner)
            guard(frames[i][1], body)
        out_home(g).wait()
        out_away(g).wait_send()
        out_arrived(g).wait_recv()
        return 0

    run(0, full_chunks, drain, FULL)
    run(full_chunks, reach_chunks, drain, CROSS)
    run(reach_chunks, chunks, drain, NEAR)

    for h in range(heads):
        spot = rank[h]
        out_ref[:, h * DH : (h + 1) * DH] = owhole[spot & 1, spot >> 1]


def solution(mesh):
    n_tm, n_height = mesh.shape["tm"], mesh.shape["height"]

    def per_device(queries, keys, values, windows, tile_mask, coefficient, layer, steering):
        frames, rows, cols, tile, features = queries.shape
        heads = features // DH
        tokens = frames * rows * cols * tile
        chunks = heads // 2 // HC
        cw = HC * DH
        span = 2 * tokens
        nr = min(n_height, 3)
        ns = 3 * nr
        flat = (tokens, features)
        hbm = pl.BlockSpec(memory_space=pltpu.MemorySpace.HBM)
        vmem = pl.BlockSpec(memory_space=pltpu.VMEM)
        smem = pl.BlockSpec(memory_space=pltpu.SMEM)
        bf16 = jnp.bfloat16
        offsets = tile_mask.shape[-1]
        packed = pltpu.VMEM((chunks, 2, tokens, cw), bf16)

        def attention(number, full_chunks, reach_chunks):
            return pl.pallas_call(
                functools.partial(kernel, n_tm, n_height, heads, full_chunks, reach_chunks),
                out_shape=jax.ShapeDtypeStruct(flat, bf16),
                in_specs=[hbm, hbm, hbm, smem, hbm, smem, smem, hbm],
                out_specs=vmem,
                scratch_shapes=[
                    pltpu.VMEM((ns, chunks, 2, tokens, cw), bf16),
                    pltpu.VMEM((ns, chunks, 2, tokens, cw), bf16),
                    packed,
                    pltpu.VMEM((cols, offsets), jnp.int32),
                    pltpu.VMEM((2 * ns + 1, span, span), jnp.float32),
                    pltpu.VMEM((ns, span, span), jnp.float32),
                    pltpu.VMEM((heads, 1, DH), jnp.float32),
                    pltpu.VMEM((chunks, 2, HC, tokens, DH), bf16),
                    pltpu.VMEM((3, tokens, features), bf16),
                    pltpu.VMEM((3, heads, tokens, DH), bf16),
                    packed,
                    packed,
                    packed,
                    pltpu.VMEM((2, chunks * HC, tokens, DH), bf16),
                    pltpu.VMEM((cols, offsets), jnp.int32),
                    pltpu.VMEM(steering.shape, bf16),
                    pltpu.SMEM((heads,), jnp.int32),
                    pltpu.SMEM((heads,), jnp.int32),
                    pltpu.SemaphoreType.DMA((2, 3 * nr, chunks, 2)),
                    pltpu.SemaphoreType.DMA((2, ns, chunks, 2)),
                    pltpu.SemaphoreType.DMA((4, chunks)),
                    pltpu.SemaphoreType.DMA((2, chunks)),
                    pltpu.SemaphoreType.DMA((2,)),
                    pltpu.SemaphoreType.DMA((2, chunks)),
                    pltpu.SemaphoreType.DMA((5,)),
                ],
                compiler_params=pltpu.CompilerParams(
                    collective_id=number, has_side_effects=True, vmem_limit_bytes=48 * 1024 * 1024
                ),
            )

        plans = [(5, 5), (4, 6), (4, 7), (6, 6), (5, 8), (7, 7)]
        plans = [plan for plan in plans if plan[1] < chunks] + [(chunks, chunks)]
        along = windows[:, 0] >= 1
        both = along & (windows[:, 1] >= 1)
        counts = jnp.sum(along.astype(jnp.int32) * 64 + both.astype(jnp.int32))
        n_along, n_both = counts >> 6, counts & 63
        choice = jnp.int32(len(plans) - 1)
        for n, (full, reach) in reversed(list(enumerate(plans[:-1]))):
            fits = (n_both <= 2 * HC * full) & (n_along <= 2 * HC * reach)
            choice = jnp.where(fits, n, choice)
        out = lax.switch(
            choice,
            [attention(n, *plan) for n, plan in enumerate(plans)],
            queries.reshape(flat), keys.reshape(flat), values.reshape(flat), windows.T,
            tile_mask.reshape(cols, offsets), coefficient, layer, steering,
        )
        return out.reshape(queries.shape)

    tiles = P(("sweep", "tm"), "height", "width", None, None)
    return jax.shard_map(
        per_device,
        mesh=mesh,
        in_specs=(tiles, tiles, tiles, P(), P("tm", "height", "width", None), P("sweep"), P("sweep"), P()),
        out_specs=tiles,
        check_vma=False,
    )
```

```python
import functools
import math

import jax
import jax.numpy as jnp
from jax import lax
from jax.experimental import pallas as pl
from jax.experimental.pallas import tpu as pltpu
from jax.sharding import PartitionSpec as P

DH = 128
NEG = -1e30
MESH = pl.DeviceIdType.MESH
HC = 1
FULL, CROSS, NEAR, SELF = range(4)


def kernel(
    n_tm, n_height, heads, full_chunks, reach_chunks, row_chunks,
    q_hbm, k_hbm, v_hbm, win_ref, mask_hbm, coef_ref, layer_ref, steer_hbm,
    out_ref,
    kbuf, vbuf, qbuf, mbuf, bias, scores, svec, ostage,
    raw, byhead, q_ref, k_ref, v_ref, owhole, mask_ref, steer_ref, rank, perm,
    ssem, rsem, lsem, qsem, msem, osem, isem,
):
    tokens = raw.shape[1]
    cols = mask_ref.shape[0]
    tile = tokens // cols
    all_cols = 2 * cols
    half = (heads // 2) * DH
    cw = HC * DH
    chunks = half // cw
    c = lax.axis_index("width")
    z = lax.axis_index("tm")
    x = lax.axis_index("height")
    sib = 1 - c
    if n_height == 1:
        rows = []
    elif n_height == 2:
        rows = [(1 - 2 * x, True, 1)]
    else:
        rows = [(-1, x > 0, 2), (1, x < n_height - 1, 1)]
    nr = 1 + len(rows)
    ns = 3 * nr
    frames = [(-1, z > 0, 2), (1, z < n_tm - 1, 1)]
    bufs = ((k_ref, kbuf), (v_ref, vbuf))

    def guard(cond, body):
        if cond is True:
            body()
        else:
            pl.when(cond)(body)

    loads = [
        pltpu.make_async_copy(src, raw.at[i], isem.at[i])
        for i, src in enumerate((k_hbm, v_hbm, q_hbm))
    ]
    loads.append(pltpu.make_async_copy(mask_hbm, mask_ref, isem.at[3]))
    loads.append(pltpu.make_async_copy(steer_hbm, steer_ref, isem.at[4]))
    for load in loads:
        load.start()

    barrier = pltpu.get_barrier_semaphore()

    def greet(**where):
        pl.semaphore_signal(barrier, inc=1, device_id=where, device_id_type=MESH)

    greet(width=sib)
    expect = jnp.int32(1)
    for d, ok, _ in rows:
        def body(d=d):
            for t in range(2):
                greet(height=x + d, width=jnp.int32(t))
        guard(ok, body)
        expect = expect + (2 if ok is True else 2 * ok.astype(jnp.int32))
    for d, ok, _ in frames:
        def body(d=d):
            for t in range(2):
                greet(tm=z + d, width=jnp.int32(t))
        guard(ok, body)
        expect = expect + 2 * ok.astype(jnp.int32)

    along = [jnp.where(win_ref[0, h] >= 1, 1, 0) for h in range(heads)]
    both = [along[h] * jnp.where(win_ref[1, h] >= 1, 1, 0) for h in range(heads)]
    n_along = functools.reduce(lambda a, b: a + b, along)
    n_both = functools.reduce(lambda a, b: a + b, both)
    over = [(1 - along[h]) * jnp.where(win_ref[1, h] >= 1, 1, 0) for h in range(heads)]
    n_over = functools.reduce(lambda a, b: a + b, over)
    place_both, place_along = jnp.int32(0), n_both
    place_over, place_rest = n_along, n_along + n_over
    for h in range(heads):
        rank[h] = jnp.where(
            both[h] == 1,
            place_both,
            jnp.where(
                along[h] == 1, place_along, jnp.where(over[h] == 1, place_over, place_rest)
            ),
        )
        place_both = place_both + both[h]
        place_along = place_along + along[h] - both[h]
        place_over = place_over + over[h]
        place_rest = place_rest + 1 - along[h] - over[h]

    def invert(i, _):
        head = jnp.int32(0)
        for h in range(heads):
            head = jnp.where(rank[h] == i, h, head)
        perm[i] = head
        return 0

    lax.fori_loop(0, heads, invert, 0)

    def pack(which, ref):
        loads[which].wait()
        for h in range(heads):
            byhead[which, h] = raw[which, :, h * DH : (h + 1) * DH]

        def one(g, _):
            for core in range(2):
                for hh in range(HC):
                    head = perm[(g * HC + hh) * 2 + core]
                    ref[g, core, :, hh * DH : (hh + 1) * DH] = byhead[which, head]
            return 0

        lax.fori_loop(0, chunks, one, 0)

    pack(0, k_ref)
    pack(1, v_ref)
    pl.semaphore_wait(barrier, expect)

    def remote(src, dst, s, r, where):
        return pltpu.make_async_remote_copy(
            src_ref=src, dst_ref=dst, send_sem=s, recv_sem=r, device_id=where, device_id_type=MESH
        )

    def own(kv, dest, g, core, slot, where):
        src, buf = bufs[kv]
        return remote(
            src.at[g, core], buf.at[slot, g, c],
            ssem.at[kv, dest, g, core], rsem.at[kv, slot, g, c], where,
        )

    def to_sibling(kv, g):
        return own(kv, 0, g, sib, 0, dict(width=sib))

    def to_row(kv, i, g, core):
        d, _, there = rows[i]
        return own(kv, 1 + i, g, jnp.int32(core), there, dict(height=x + d, width=jnp.int32(core)))

    def to_frame(kv, i, g, core):
        d, _, there = frames[i]
        return own(kv, nr + i, g, jnp.int32(core), there * nr, dict(tm=z + d, width=jnp.int32(core)))

    def forward(kv, j, i, g):
        d, _, there = frames[i]
        buf = bufs[kv][1]
        return remote(
            buf.at[1 + j, g], buf.at[there * nr + 1 + j, g],
            ssem.at[kv, nr + 2 + 2 * j + i, g, 0], rsem.at[kv, there * nr + 1 + j, g, 0],
            dict(tm=z + d),
        )

    def arrived(kv, slot, g, core):
        src, buf = bufs[kv]
        return remote(
            src.at[g, core], buf.at[slot, g, core],
            ssem.at[kv, 0, g, core], rsem.at[kv, slot, g, core], dict(width=sib),
        )

    def forwarded(kv, slot, g):
        buf = bufs[kv][1]
        return remote(
            buf.at[slot, g], buf.at[slot, g],
            ssem.at[kv, 0, g, 0], rsem.at[kv, slot, g, 0], dict(width=sib),
        )

    def keep(kv, g):
        src, buf = bufs[kv]
        return pltpu.make_async_copy(src.at[g, c], buf.at[0, g, c], lsem.at[kv, g])

    def keep_q(g):
        return pltpu.make_async_copy(q_ref.at[g, c], qbuf.at[g, c], lsem.at[2, g])

    def send_q(g):
        return remote(
            q_ref.at[g, sib], qbuf.at[g, c], qsem.at[0, g], qsem.at[1, g], dict(width=sib)
        )

    def send_mask():
        return remote(mask_hbm, mbuf, msem.at[0], msem.at[1], dict(width=sib))

    def row_ok(i):
        return rows[i][1]

    send_mask().start()

    def start_rows(g, _):
        for i in range(nr - 1):
            def body(i=i):
                for core in range(2):
                    for kv in range(2):
                        to_row(kv, i, g, core).start()
            guard(row_ok(i), body)
        return 0

    def start_frames(g):
        for i in range(2):
            def body(i=i):
                for core in range(2):
                    for kv in range(2):
                        to_frame(kv, i, g, core).start()
            guard(frames[i][1], body)

    def start_local(g, _):
        keep_q(g).start()
        send_q(g).start()
        for kv in range(2):
            keep(kv, g).start()
            to_sibling(kv, g).start()
        return 0

    start_rows(0, 0)
    start_frames(0)
    lax.fori_loop(1, row_chunks, start_rows, 0)
    pack(2, q_ref)
    lax.fori_loop(0, chunks, start_local, 0)
    loads[3].wait()
    loads[4].wait()

    for i in range(nr - 1):
        if row_ok(i) is not True:
            @pl.when(jnp.logical_not(row_ok(i)))
            def _(i=i):
                for f in range(3):
                    for _, buf in bufs:
                        buf[f * nr + 1 + i] = jnp.zeros(buf.shape[1:], buf.dtype)
    for i in range(2):
        @pl.when(jnp.logical_not(frames[i][1]))
        def _(i=i):
            for j in range(nr):
                for _, buf in bufs:
                    def zero(g, _, j=j, buf=buf):
                        buf[(1 + i) * nr + j, g] = jnp.zeros(buf.shape[2:], buf.dtype)
                        return 0
                    count = reach_chunks if j == 0 else full_chunks
                    if j == 0 or row_ok(j - 1) is True:
                        lax.fori_loop(0, count, zero, 0)
                    else:
                        @pl.when(row_ok(j - 1))
                        def _(zero=zero, count=count):
                            lax.fori_loop(0, count, zero, 0)

    pick = lax.broadcasted_iota(jnp.int32, (steer_ref.shape[0], DH), 0) == layer_ref[0]
    for h in range(heads):
        rows_f32 = steer_ref[:, h * DH : (h + 1) * DH].astype(jnp.float32)
        svec[h] = coef_ref[0] * jnp.sum(jnp.where(pick, rows_f32, 0.0), axis=0, keepdims=True)

    def pump(g, _):
        @pl.when(g > 0)
        def _():
            start_frames(g)
        for j in range(nr - 1):
            def body(j=j):
                for core in range(2):
                    for kv in range(2):
                        arrived(kv, 1 + j, g, jnp.int32(core)).wait_recv()
                for i in range(2):
                    def inner(i=i):
                        for kv in range(2):
                            forward(kv, j, i, g).start()
                    guard(frames[i][1], inner)
            guard(row_ok(j), body)
        return 0

    lax.fori_loop(0, full_chunks, pump, 0)

    def straight(g, _):
        start_frames(g)
        return 0

    if full_chunks < reach_chunks:
        lax.fori_loop(full_chunks, reach_chunks, straight, 0)

    send_mask().wait_recv()
    theirs = mbuf[...]
    mine = mask_ref[...]
    first = jnp.where(c == 0, mine, theirs)
    second = jnp.where(c == 0, theirs, mine)
    kept = jnp.concatenate([first, second], axis=0)
    span = all_cols * tile
    lane = lax.broadcasted_iota(jnp.int32, (1, kept.shape[1]), 1)
    block = lax.broadcasted_iota(jnp.int32, (1, span), 1) // tile
    for f in range(3):
        df = (0, -1, 1)[f]
        f_ok = True if f == 0 else frames[f - 1][1]
        for r in range(nr):
            dr = 0 if r == 0 else rows[r - 1][0]
            r_ok = True if r == 0 else row_ok(r - 1)
            base = 9 * (df + 1) + 3 * (dr + 1)
            slot = f * nr + r
            ok = None
            for cond in (f_ok, r_ok):
                if cond is not True:
                    ok = cond if ok is None else jnp.logical_and(ok, cond)
            for qc in range(all_cols):
                line = jnp.full((1, span), NEG, jnp.float32)
                for kc in range(max(qc - 1, 0), min(qc + 2, all_cols)):
                    if slot == 0 and kc == qc:
                        value = jnp.zeros((1, 1), jnp.float32)
                    else:
                        here = jnp.where(lane == base + (kc - qc + 1), kept[qc : qc + 1], 0)
                        hit = jnp.sum(here.astype(jnp.float32), axis=1, keepdims=True)
                        value = jnp.where(hit == 1.0, 0.0, NEG)
                        if ok is not None:
                            value = jnp.where(ok, value, NEG)
                    line = jnp.where(block == kc, value, line)
                alone = jnp.where(block == qc, line, NEG)
                at = pl.ds(qc * tile, tile)
                bias[slot, at, :] = jnp.broadcast_to(alone, (tile, span))
                bias[ns + slot, at, :] = jnp.broadcast_to(line, (tile, span))
    bias[2 * ns] = jnp.full((span, span), NEG, jnp.float32)

    scale = 1.0 / math.sqrt(DH)

    def place(core, g):
        return owhole.at[core, pl.ds(g * HC, HC)]

    def out_home(g):
        return pltpu.make_async_copy(ostage.at[g, c], place(c, g), lsem.at[3, g])

    def out_away(g):
        return remote(
            ostage.at[g, sib], place(c, g), osem.at[0, g], osem.at[1, g], dict(width=sib)
        )

    def out_arrived(g):
        return remote(
            ostage.at[g, sib], place(sib, g), osem.at[0, g], osem.at[1, g], dict(width=sib)
        )

    def attend(kind, g, _):
        slots = [
            slot for slot in range(ns)
            if slot == 0 or kind == FULL or (slot < nr and kind != SELF)
            or (kind == CROSS and slot % nr == 0)
        ]
        keep_q(g).wait()
        send_q(g).wait_recv()
        for kv in range(2):
            keep(kv, g).wait()
            arrived(kv, 0, g, sib).wait_recv()
        if kind in (CROSS, NEAR):
            for j in range(nr - 1):
                def near(j=j):
                    for core in range(2):
                        for kv in range(2):
                            arrived(kv, 1 + j, g, jnp.int32(core)).wait_recv()
                guard(row_ok(j), near)
        for i in range(2 if kind in (FULL, CROSS) else 0):
            def body(i=i):
                for kv in range(2):
                    for core in range(2):
                        arrived(kv, (1 + i) * nr, g, jnp.int32(core)).wait_recv()
                    for j in range(nr - 1 if kind == FULL else 0):
                        def inner(j=j, kv=kv):
                            forwarded(kv, (1 + i) * nr + 1 + j, g).wait_recv()
                        guard(row_ok(j), inner)
            guard(frames[i][1], body)
        for hh in range(HC):
            h = perm[(g * HC + hh) * 2 + c]
            lanes = slice(hh * DH, (hh + 1) * DH)
            wf, wr, wc = win_ref[0, h], win_ref[1, h], win_ref[2, h]
            q = qbuf[g][:, :, lanes].reshape(span, DH)
            top = None
            for slot in slots:
                index = jnp.where(wc >= 1, ns + slot, slot)
                if slot // nr > 0:
                    index = jnp.where(wf >= 1, index, 2 * ns)
                if slot % nr > 0:
                    index = jnp.where(wr >= 1, index, 2 * ns)
                key = kbuf[slot, g][:, :, lanes].reshape(span, DH)
                s = lax.dot_general(
                    q, key, (((1,), (1,)), ((), ())), preferred_element_type=jnp.float32
                )
                s = s * scale + bias[index]
                scores[slot] = s
                high = jnp.maximum(s[:, :DH], s[:, DH:]) if span == 2 * DH else jnp.max(s, axis=1, keepdims=True)
                top = high if top is None else jnp.maximum(top, high)
            top = jnp.max(top, axis=1, keepdims=True)
            total = None
            mixture = None
            for slot in slots:
                e = jnp.exp(scores[slot] - top)
                part = e[:, :DH] + e[:, DH:] if span == 2 * DH else jnp.sum(e, axis=1, keepdims=True)
                total = part if total is None else total + part
                value = vbuf[slot, g][:, :, lanes].reshape(span, DH)
                term = jnp.dot(e.astype(jnp.bfloat16), value, preferred_element_type=jnp.float32)
                mixture = term if mixture is None else mixture + term
            total = jnp.sum(total, axis=1, keepdims=True)
            attended = mixture * (1.0 / total) + svec[h]
            attended = attended.astype(ostage.dtype)
            ostage[g, 0, hh] = attended[:tokens]
            ostage[g, 1, hh] = attended[tokens:]
        out_home(g).start()
        out_away(g).start()
        return 0

    def run(start, stop, step, kind):
        if start < stop:
            lax.fori_loop(start, stop, functools.partial(step, kind), 0)

    run(row_chunks, chunks, attend, SELF)
    if full_chunks == reach_chunks and 2 * full_chunks > chunks:
        run(reach_chunks, row_chunks, attend, NEAR)
        run(0, full_chunks, attend, FULL)
    else:
        run(0, full_chunks, attend, FULL)
        run(reach_chunks, row_chunks, attend, NEAR)
        run(full_chunks, reach_chunks, attend, CROSS)

    send_mask().wait_send()

    def drain(kind, g, _):
        send_q(g).wait_send()
        for kv in range(2):
            to_sibling(kv, g).wait_send()
        for i in range(nr - 1 if kind != SELF else 0):
            def body(i=i):
                for core in range(2):
                    for kv in range(2):
                        to_row(kv, i, g, core).wait_send()
            guard(row_ok(i), body)
        for i in range(2 if kind in (FULL, CROSS) else 0):
            def body(i=i):
                for kv in range(2):
                    for core in range(2):
                        to_frame(kv, i, g, core).wait_send()
                    for j in range(nr - 1 if kind == FULL else 0):
                        def inner(j=j, kv=kv):
                            forward(kv, j, i, g).wait_send()
                        guard(row_ok(j), inner)
            guard(frames[i][1], body)
        out_home(g).wait()
        out_away(g).wait_send()
        out_arrived(g).wait_recv()
        return 0

    run(0, full_chunks, drain, FULL)
    run(full_chunks, reach_chunks, drain, CROSS)
    run(reach_chunks, row_chunks, drain, NEAR)
    run(row_chunks, chunks, drain, SELF)

    for h in range(heads):
        spot = rank[h]
        out_ref[:, h * DH : (h + 1) * DH] = owhole[spot & 1, spot >> 1]


def solution(mesh):
    n_tm, n_height = mesh.shape["tm"], mesh.shape["height"]

    def per_device(queries, keys, values, windows, tile_mask, coefficient, layer, steering):
        frames, rows, cols, tile, features = queries.shape
        heads = features // DH
        tokens = frames * rows * cols * tile
        chunks = heads // 2 // HC
        cw = HC * DH
        span = 2 * tokens
        nr = min(n_height, 3)
        ns = 3 * nr
        flat = (tokens, features)
        hbm = pl.BlockSpec(memory_space=pltpu.MemorySpace.HBM)
        vmem = pl.BlockSpec(memory_space=pltpu.VMEM)
        smem = pl.BlockSpec(memory_space=pltpu.SMEM)
        bf16 = jnp.bfloat16
        offsets = tile_mask.shape[-1]
        packed = pltpu.VMEM((chunks, 2, tokens, cw), bf16)

        def attention(number, *plan):
            return pl.pallas_call(
                functools.partial(kernel, n_tm, n_height, heads, *plan),
                out_shape=jax.ShapeDtypeStruct(flat, bf16),
                in_specs=[hbm, hbm, hbm, smem, hbm, smem, smem, hbm],
                out_specs=vmem,
                scratch_shapes=[
                    pltpu.VMEM((ns, chunks, 2, tokens, cw), bf16),
                    pltpu.VMEM((ns, chunks, 2, tokens, cw), bf16),
                    packed,
                    pltpu.VMEM((cols, offsets), jnp.int32),
                    pltpu.VMEM((2 * ns + 1, span, span), jnp.float32),
                    pltpu.VMEM((ns, span, span), jnp.float32),
                    pltpu.VMEM((heads, 1, DH), jnp.float32),
                    pltpu.VMEM((chunks, 2, HC, tokens, DH), bf16),
                    pltpu.VMEM((3, tokens, features), bf16),
                    pltpu.VMEM((3, heads, tokens, DH), bf16),
                    packed,
                    packed,
                    packed,
                    pltpu.VMEM((2, chunks * HC, tokens, DH), bf16),
                    pltpu.VMEM((cols, offsets), jnp.int32),
                    pltpu.VMEM(steering.shape, bf16),
                    pltpu.SMEM((heads,), jnp.int32),
                    pltpu.SMEM((heads,), jnp.int32),
                    pltpu.SemaphoreType.DMA((2, 3 * nr, chunks, 2)),
                    pltpu.SemaphoreType.DMA((2, ns, chunks, 2)),
                    pltpu.SemaphoreType.DMA((4, chunks)),
                    pltpu.SemaphoreType.DMA((2, chunks)),
                    pltpu.SemaphoreType.DMA((2,)),
                    pltpu.SemaphoreType.DMA((2, chunks)),
                    pltpu.SemaphoreType.DMA((5,)),
                ],
                compiler_params=pltpu.CompilerParams(
                    collective_id=number, has_side_effects=True, vmem_limit_bytes=48 * 1024 * 1024
                ),
            )

        plans = [(5, 5, 8), (4, 6, 8), (5, 7, 8), (5, 5, 10), (5, 7, 10), (6, 8, 10)]
        plans = [plan for plan in plans if plan[1] < chunks and plan[2] <= chunks]
        plans.append((chunks, chunks, chunks))
        along = windows[:, 0] >= 1
        over = windows[:, 1] >= 1
        counts = jnp.sum(jnp.where(along, 4096, 0) + jnp.where(along & over, 64, 0) + jnp.where(along | over, 1, 0))
        n_along, n_both, n_either = counts >> 12, (counts >> 6) & 63, counts & 63
        choice = jnp.int32(len(plans) - 1)
        for n, (full, reach, row) in reversed(list(enumerate(plans[:-1]))):
            fits = (n_both <= 2 * HC * full) & (n_along <= 2 * HC * reach) & (n_either <= 2 * HC * row)
            choice = jnp.where(fits, n, choice)
        out = lax.switch(
            choice,
            [attention(n, *plan) for n, plan in enumerate(plans)],
            queries.reshape(flat), keys.reshape(flat), values.reshape(flat), windows.T,
            tile_mask.reshape(cols, offsets), coefficient, layer, steering,
        )
        return out.reshape(queries.shape)

    tiles = P(("sweep", "tm"), "height", "width", None, None)
    return jax.shard_map(
        per_device,
        mesh=mesh,
        in_specs=(tiles, tiles, tiles, P(), P("tm", "height", "width", None), P("sweep"), P("sweep"), P()),
        out_specs=tiles,
        check_vma=False,
    )
```
